512 devices in a mesh: claims: 16 (over y, core), feat: 32 (over z, x).
Axes of the slice: x: 4, y: 8, z: 8, core: 2. Of those that a mesh axis runs over, the one named last changes fastest.
Arguments:
- design: bfloat16 [32768, 16384], P('claims', 'feat'), may hold values from -0.09375 to 0.09375
- irls_weights: float32 [32768], P('claims'), may hold values from 0.2 to 5
- ridge_diag: float32 [16384], P('feat'), may hold values from 0.5 to 2
- gradients: float32 [16384, 8], P('feat'), may hold values from -45 to 45
Outputs:
- solution: float32 [16384, 8], P('feat')
- residual: float32 [16384, 8], P('feat')
The draws below stay inside these ranges and needn't reach their ends.
All inputs are finite; a program needn't handle non-finite values.
Results may differ from the reference program's by a relative error of at most 0.0085.
Values may be sent and summed in bfloat16 or wider, within the bound.
A program may use at most 64 MiB of HBM per device.

```python
import math
import jax
import jax.numpy as jnp
from jax import lax

F = 16384
K = 8
ITERS = 2
ROWS = 32768


def draw_gradients(key, part):
    key_one, key_two = jax.random.split(key, 2)
    rising = jnp.exp(jnp.log(3.0) * jnp.arange(F, dtype=jnp.float32) / F)[:, None]
    column_scale = jnp.exp(jax.random.uniform(key_two, (1, K), jnp.float32, 0.0, jnp.log(10.0)))
    values = jax.random.normal(key_one, (F, K), jnp.float32)
    values = jnp.clip(values, -5.0, 5.0)
    return 0.3 * values * rising * column_scale


def strengthened(array, rng, source, target, shards_of, factor):
    owner, partner = [(jnp.arange(array.shape[axis_at]) // (array.shape[axis_at] // shards_of)).reshape([-1 if axis == axis_at else 1 for axis in range(array.ndim)]) for axis_at in (source, target)]
    chosen = jax.random.permutation(rng, shards_of)[partner]
    strong = (owner == chosen) | (owner == (partner + shards_of // 2) % shards_of)
    return jnp.where(strong, factor * array, array)


def level_of(stream_key, dims, shards, least, top_value):
    factor_of = 1.0
    for axis_at, parts in shards:
        steps = jax.random.uniform(jax.random.fold_in(jax.random.fold_in(stream_key, 6), axis_at), (parts,), jnp.float32, least / len(shards), top_value / len(shards))
        factor_of = factor_of * jnp.repeat(jnp.exp(steps), dims[axis_at] // parts).reshape((-1,) + (1,) * (len(dims) - 1 - axis_at))
    return factor_of


def heavy_noise(stream_key, extent, spread, limit, pieces, heavy, kind=jnp.bfloat16):
    values = spread * jax.random.normal(stream_key, extent, jnp.float32)
    if pieces:
        values = values * level_of(stream_key, extent, pieces, -0.22, 0.18)
    return jnp.clip(strengthened(values, jax.random.fold_in(stream_key, 3), *heavy), -limit, limit).astype(kind)


def setup_inputs(seed: int = 0) -> dict:
    key_of = jax.random.split(jax.random.key(seed), 5)
    design = heavy_noise(key_of[0], (ROWS, F), F ** -0.5, 0.09375, ((0, 16), (1, 32)), (0, 1, 32, 2.75))
    irls_weights = jnp.clip(jnp.exp(math.log(5.0) - 3.218876 * jax.random.uniform(key_of[1], (ROWS,), jnp.float32) ** level_of(key_of[1], (ROWS,), ((0, 16),), -0.2, 0.2)), 0.2, 5.0)
    ridge_diag = jnp.clip(jnp.exp(math.log(2.0) - 1.3862944 * jax.random.uniform(key_of[2], (F,), jnp.float32) ** level_of(key_of[2], (F,), ((0, 32),), -0.2, 0.2)), 0.5, 2.0)
    gradients = draw_gradients(jax.random.fold_in(key_of[4], 71), 0)
    return dict(design=design, irls_weights=irls_weights, ridge_diag=ridge_diag, gradients=gradients)


def reference(design, irls_weights, ridge_diag, gradients):
    solution = jnp.zeros_like(gradients)
    residual = gradients
    direction = gradients
    norm_now = jnp.sum(residual * residual, axis=0)
    for loop_step in range(ITERS):
        dir_half = direction.astype(jnp.bfloat16)
        row_values = jnp.dot(design, dir_half, preferred_element_type=jnp.float32)
        scaled_rows = (irls_weights[:, None] * row_values).astype(jnp.bfloat16)
        hess_image = lax.dot_general(design, scaled_rows, (((0,), (0,)), ((), ())), preferred_element_type=jnp.float32)
        hess_image = hess_image + ridge_diag[:, None] * direction
        step_size = norm_now / jnp.sum(direction * hess_image, axis=0)
        solution = solution + step_size * direction
        residual = residual - step_size * hess_image
        norm_next = jnp.sum(residual * residual, axis=0)
        direction = residual + (norm_next / norm_now) * direction
        norm_now = norm_next
    return solution, residual
```

```python
import functools

import jax
import jax.numpy as jnp
from jax import lax
from jax.experimental import pallas as pl
from jax.experimental.pallas import tpu as pltpu
from jax.sharding import PartitionSpec as P

MESH = pl.DeviceIdType.MESH
BF16, F32 = jnp.bfloat16, jnp.float32
NX, NZ, NY = 4, 8, 8
K = 8
ROWS_LOCAL, WIDTH = 2048, 512
SEG = ROWS_LOCAL // 4
HALF = WIDTH // 2
ZS = (4, 3, 5, 2, 6, 1, 7)
NT = (((1,), (1,)), ((), ()))


def kernel(
    x_hbm, w_hbm, rd_hbm, g_hbm, sol_ref, res_ref,
    xv, wv, rdv, gv, y_opp, y_in, z_in, h_in, s_in,
    q_src, qz_in, qx_in, qy_in, qc_in,
    load_sem, xsem, send_sem, recv_sem,
):
    c, f = lax.axis_index("claims"), lax.axis_index("feat")
    y, core = c // 2, lax.rem(c, 2)
    z, x = f // NX, lax.rem(f, NX)
    par = lax.rem(z, 2)
    opp = 1 - par
    slot = par * NX + x
    z_pair = z + 1 - 2 * par
    c_pair = c + 1 - 2 * core

    loads = [
        pltpu.make_async_copy(src, dst, load_sem.at[i])
        for i, (src, dst) in enumerate(((g_hbm, gv), (rd_hbm, rdv), (w_hbm, wv)))
    ]
    loads[0].start()

    def x_load(seg):
        rows = pl.ds(pl.multiple_of(seg * SEG, SEG), SEG)
        return pltpu.make_async_copy(x_hbm.at[rows], xv.at[rows], xsem.at[seg])

    seg_order = (2 * par, 2 * par + 1, 2 * opp, 2 * opp + 1)
    for seg in seg_order:
        x_load(seg).start()
    loads[1].start()
    loads[2].start()

    barrier = pltpu.get_barrier_semaphore()
    z_peers = [lax.rem(z + k, NZ) * NX + x for k in ZS]
    x_peers = [z * NX + lax.rem(x + k, NX) for k in (2, 1, 3)]
    d_peers = [z_pair * NX + lax.rem(x + k, NX) for k in (2, 1, 3, 0)]
    y_peers = [lax.rem(y + k, NY) * 2 + core for k in ZS]
    for peer in z_peers + x_peers + d_peers[:3]:
        pl.semaphore_signal(barrier, 1, device_id={"feat": peer}, device_id_type=MESH)
    for peer in y_peers + [c_pair]:
        pl.semaphore_signal(barrier, 1, device_id={"claims": peer}, device_id_type=MESH)

    lane = lax.broadcasted_iota(jnp.int32, (K, 128), 1)
    sub = lax.broadcasted_iota(jnp.int32, (K, 128), 0)

    def to_row(*columns):
        tile = jnp.zeros((K, 128), F32)
        for j, column in enumerate(columns):
            tile = jnp.where(lane == sub + K * j, column, tile)
        return jnp.sum(tile, axis=0, keepdims=True)

    def from_row(row, j):
        return jnp.sum(jnp.where(lane == sub + K * j, row, 0.0), axis=1, keepdims=True)

    def send(src, dst, it, kind, device):
        pltpu.make_async_remote_copy(
            src, dst, send_sem.at[it, kind], recv_sem.at[it, kind],
            device_id=device, device_id_type=MESH,
        ).start()

    def arrived(ref, it, kind):
        pltpu.make_async_copy(ref, ref, recv_sem.at[it, kind]).wait()

    def row_seg(seg):
        return pl.ds(pl.multiple_of(seg * SEG, SEG), SEG)

    def feat_sum(it, product, columns):
        for own, half in ((True, par), (False, opp)):
            block = jnp.concatenate([product(2 * half), product(2 * half + 1)], axis=0).astype(BF16)
            if own:
                y_in[it, z] = block
                if it == 0:
                    pl.semaphore_wait(barrier, 21)
            else:
                y_opp[it] = block
            for k, peer in zip(ZS, z_peers):
                if (k % 2 == 0) == own:
                    send(y_in.at[it, z] if own else y_opp.at[it], y_in.at[it, z], it, 0, {"feat": peer})
        qz_in[it, z] = to_row(*columns)
        for peer in z_peers:
            send(qz_in.at[it, z], qz_in.at[it, z], it, 1, {"feat": peer})
        arrived(y_in.at[it, pl.ds(0, NZ - 1)], it, 0)
        total = y_in[it, 0].astype(F32)
        for j in range(1, NZ):
            total += y_in[it, j].astype(F32)
        z_in[it, slot] = total.astype(BF16)
        for near, far in zip(x_peers, d_peers):
            send(z_in.at[it, slot], z_in.at[it, slot], it, 2, {"feat": far})
            send(z_in.at[it, slot], z_in.at[it, slot], it, 2, {"feat": near})
        send(z_in.at[it, slot], z_in.at[it, slot], it, 2, {"feat": d_peers[3]})
        arrived(qz_in.at[it, pl.ds(0, NZ - 1)], it, 1)
        qx_in[it, x] = jnp.sum(qz_in[it], axis=0)
        for peer in x_peers:
            send(qx_in.at[it, x], qx_in.at[it, x], it, 3, {"feat": peer})
        arrived(qx_in.at[it, pl.ds(0, NX - 1)], it, 3)
        row = jnp.sum(qx_in[it], axis=0)
        arrived(z_in.at[it, pl.ds(0, 2 * NX - 1)], it, 2)
        halves = []
        for half in range(2):
            total = z_in[it, half * NX].astype(F32)
            for j in range(1, NX):
                total += z_in[it, half * NX + j].astype(F32)
            halves.append(total)
        return halves, row

    def claims_sum(it, halves):
        image = jnp.zeros((K, WIDTH), F32)
        energy = jnp.zeros((K, SEG), F32)
        for half in range(2):
            for s in range(2):
                seg = 2 * half + s
                values = halves[half][K * s:K * (s + 1)]
                weighted = wv[:, seg * SEG:(seg + 1) * SEG] * values
                energy += weighted * values
                image += jnp.dot(weighted.astype(BF16), xv[seg * SEG:(seg + 1) * SEG, :],
                                 preferred_element_type=F32)
        h_in[it, y] = jnp.concatenate([image[:, :HALF], image[:, HALF:]], axis=0).astype(BF16)
        for peer in y_peers:
            send(h_in.at[it, y], h_in.at[it, y], it, 4, {"claims": peer})
        qy_in[it, y] = to_row(jnp.sum(energy, axis=1, keepdims=True))
        for peer in y_peers:
            send(qy_in.at[it, y], qy_in.at[it, y], it, 5, {"claims": peer})
        arrived(h_in.at[it, pl.ds(0, NY - 1)], it, 4)
        total = h_in[it, 0].astype(F32)
        for j in range(1, NY):
            total += h_in[it, j].astype(F32)
        s_in[it, core] = total
        send(s_in.at[it, core], s_in.at[it, core], it, 6, {"claims": c_pair})
        arrived(qy_in.at[it, pl.ds(0, NY - 1)], it, 5)
        qc_in[it, core] = jnp.sum(qy_in[it], axis=0)
        send(qc_in.at[it, core], qc_in.at[it, core], it, 7, {"claims": c_pair})
        arrived(s_in.at[it, 0], it, 6)
        both = s_in[it, 0] + s_in[it, 1]
        image = jnp.concatenate([both[:K], both[K:]], axis=1)
        arrived(qc_in.at[it, 0], it, 7)
        return image, from_row(qc_in[it, 0] + qc_in[it, 1], 0)

    loads[0].wait()
    grad = gv[...]
    grad_half = grad.astype(BF16)

    def first_product(seg):
        x_load(seg).wait()
        return lax.dot_general(grad_half, xv[row_seg(seg), :], NT, preferred_element_type=F32)

    loads[1].wait()
    ridge = rdv[...]
    ridge_grad = ridge * grad
    halves, row = feat_sum(
        0, first_product,
        (jnp.sum(grad * grad, axis=1, keepdims=True), jnp.sum(ridge_grad * grad, axis=1, keepdims=True)),
    )
    loads[2].wait()
    image, energy = claims_sum(0, halves)
    norm_now, ridge_gg = from_row(row, 0), from_row(row, 1)
    step_one = norm_now / (energy + ridge_gg)
    residual = grad - step_one * (image + ridge_grad)

    high = residual.astype(BF16).astype(F32)
    pair = jnp.concatenate([high, residual - high], axis=0).astype(BF16)

    def second_product(seg):
        both = lax.dot_general(pair, xv[row_seg(seg), :], NT, preferred_element_type=F32)
        return both[:K] + both[K:]

    ridge_res = ridge * residual
    res_halves, row = feat_sum(
        1, second_product,
        (
            jnp.sum(residual * residual, axis=1, keepdims=True),
            jnp.sum(ridge_res * residual, axis=1, keepdims=True),
            jnp.sum(ridge_res * grad, axis=1, keepdims=True),
        ),
    )
    norm_next = from_row(row, 0)
    beta = norm_next / norm_now
    beta_two = jnp.concatenate([beta, beta], axis=0)
    image, energy = claims_sum(1, [r + beta_two * h for r, h in zip(res_halves, halves)])
    ridge_dd = from_row(row, 1) + beta * (2.0 * from_row(row, 2) + beta * ridge_gg)
    step_two = norm_next / (energy + ridge_dd)
    direction = residual + beta * grad
    sol_ref[...] = step_one * grad + step_two * direction
    res_ref[...] = residual - step_two * (image + ridge * direction)

    for it in range(2):
        for kind, ref in (
            (0, y_in.at[it, pl.ds(0, NZ - 1)]),
            (1, qz_in.at[it, pl.ds(0, NZ - 1)]),
            (2, z_in.at[it, pl.ds(0, 2 * NX - 1)]),
            (3, qx_in.at[it, pl.ds(0, NX - 1)]),
            (4, h_in.at[it, pl.ds(0, NY - 1)]),
            (5, qy_in.at[it, pl.ds(0, NY - 1)]),
            (6, s_in.at[it, 0]),
            (7, qc_in.at[it, 0]),
        ):
            pltpu.make_async_copy(ref, ref, send_sem.at[it, kind]).wait()


def shards(design, irls_weights, ridge_diag, gradients):
    hbm = pl.BlockSpec(memory_space=pltpu.HBM)
    vmem = pl.BlockSpec(memory_space=pltpu.VMEM)
    sol, res = pl.pallas_call(
        kernel,
        out_shape=[jax.ShapeDtypeStruct((K, WIDTH), F32)] * 2,
        in_specs=[hbm] * 4,
        out_specs=[vmem] * 2,
        scratch_shapes=[
            pltpu.VMEM((ROWS_LOCAL, WIDTH), BF16),
            pltpu.VMEM((1, ROWS_LOCAL), F32),
            pltpu.VMEM((1, WIDTH), F32),
            pltpu.VMEM((K, WIDTH), F32),
            pltpu.VMEM((2, 2 * K, SEG), BF16),
            pltpu.VMEM((2, NZ, 2 * K, SEG), BF16),
            pltpu.VMEM((2, 2 * NX, 2 * K, SEG), BF16),
            pltpu.VMEM((2, NY, 2 * K, HALF), BF16),
            pltpu.VMEM((2, 2, 2 * K, HALF), F32),
            pltpu.VMEM((1, 128), F32),
            pltpu.VMEM((2, NZ, 1, 128), F32),
            pltpu.VMEM((2, NX, 1, 128), F32),
            pltpu.VMEM((2, NY, 1, 128), F32),
            pltpu.VMEM((2, 2, 1, 128), F32),
            pltpu.SemaphoreType.DMA((3,)),
            pltpu.SemaphoreType.DMA((4,)),
            pltpu.SemaphoreType.DMA((2, 8)),
            pltpu.SemaphoreType.DMA((2, 8)),
        ],
        compiler_params=pltpu.CompilerParams(collective_id=0, has_side_effects=True),
        name="cg",
    )(design, irls_weights.reshape(1, ROWS_LOCAL), ridge_diag.reshape(1, WIDTH), gradients.T)
    return sol.T, res.T


def solution(mesh):
    in_specs = (P("claims", "feat"), P("claims"), P("feat"), P("feat", None))
    out_specs = (P("feat", None), P("feat", None))
    return jax.shard_map(shards, mesh=mesh, in_specs=in_specs, out_specs=out_specs, check_vma=False)
```
